32 devices in a mesh: samp: 8 (over z, core), chan: 4 (over y, x).
Axes of the slice: x: 2, y: 2, z: 4, core: 2. Of those that a mesh axis runs over, the one named last changes fastest.
Arguments:
- out_cot: bfloat16 [8, 256, 4096], P('samp', 'chan'), may hold values from -6 to 6
- mix_weight: bfloat16 [256, 256], replicated, may hold values from -0.375 to 0.375
- corr_kernels: float32 [2, 12, 256, 64], P(None, None, 'chan'), may hold values from -0.75 to 0.75
- momentum: int32 [8], P('samp'), may hold values from 0 to 11
- spin_up: int32 [8, 4096], P('samp', 'chan'), may hold values 0 or 1
- layer_input: bfloat16 [8, 256, 4096], P('samp', None, 'chan'), may hold values from -6 to 6
- pre_one: bfloat16 [8, 256, 4096], P('samp', None, 'chan'), may hold values from -6 to 6
- pre_two: bfloat16 [8, 256, 4096], P('samp', None, 'chan'), may hold values from -6 to 6
- conv_weight: bfloat16 [3, 9, 256, 256], replicated, may hold values from -0.125 to 0.125
- dilation: int32 [3, 256], replicated, may hold values from 1 to 4, as said below
Outputs:
- input_grad: bfloat16 [8, 256, 4096], P('samp', None, 'chan')
- weight_grad: float32 [3, 9, 256, 256], P(None, None, 'chan')
The draws below stay inside these ranges and needn't reach their ends.
Inputs may be any that keep to these rules, and one draw needn't show every extreme that they name: Some channel of every convolution has dilation 4.
All inputs are finite; a program needn't handle non-finite values. No bound on the sum of `spin_up` on one device may be relied on, other than what follows from the above.
Results may differ from the reference program's by a relative error of at most 0.02.
Values may be sent and summed in bfloat16 or wider, within the bound.
A program may use at most 64 MiB of HBM per device.

```python
import math
import jax
import jax.numpy as jnp
from jax import lax

C = 256
SIDE = 64
SECTORS = 12
LAYERS = 3
MAXDIL = 4
BATCH = 8
SITES = 4096


def draw_dilation(key, part):
    key_one = jax.random.fold_in(key, 11)
    key_two = jax.random.fold_in(key, 12)
    random_base = jax.random.randint(key_one, (LAYERS, C), 1, MAXDIL + 1)
    chosen_channel = jax.random.randint(key_two, (LAYERS, 1), 0, C)
    marked = jnp.arange(C, dtype=jnp.int32)[None, :] == chosen_channel
    return jnp.where(marked, MAXDIL, random_base).astype(jnp.int32)


def touch_ends(values, own_key, smallest, high):
    shape = values.shape
    place = [jax.random.randint(jax.random.fold_in(own_key, axis), (), 0, shape[axis]) for axis in range(len(shape))]
    values = values.at[tuple(place)].set(smallest)
    longest = shape.index(max(shape))
    place[longest] = (place[longest] + 1) % shape[longest]
    return values.at[tuple(place)].set(high)


def level_of(own_key, dims, split, low, largest):
    factor_of, own = 1.0, jax.random.fold_in(own_key, 6)
    for dim, shards_of in split:
        steps = jnp.exp(jax.random.uniform(jax.random.fold_in(own, dim), (shards_of,), jnp.float32, low / len(split), largest / len(split)))
        factor_of = factor_of * jnp.repeat(steps, dims[dim] // shards_of).reshape([-1 if axis == dim else 1 for axis in range(len(dims))])
    return factor_of


def noise(key, extent, width, reach, shards=(), kind=jnp.bfloat16):
    entries = jax.random.normal(key, extent, jnp.float32) * width
    if len(shards) > 0:
        entries = level_of(key, extent, shards, -0.22, 0.18) * entries
    return jnp.clip(entries, min=-reach, max=reach).astype(kind)


def setup_inputs(seed: int = 0) -> dict:
    keys = jax.random.split(jax.random.key(seed), 11)
    return {
        "out_cot": noise(keys[0], (BATCH, C, SITES), 1.0, 6.0, ((0, 8), (1, 4))),
        "mix_weight": noise(keys[1], (C, C), C ** -0.5, 0.375),
        "corr_kernels": noise(keys[2], (2, SECTORS, C, SIDE), SIDE ** -0.5, 0.75, ((2, 4),), jnp.float32),
        "momentum": touch_ends(jax.random.randint(keys[3], (BATCH,), 0, SECTORS), jax.random.fold_in(keys[3], 1), 0, SECTORS - 1).astype(jnp.int32),
        "spin_up": touch_ends((jax.random.randint(keys[4], (BATCH, SITES), 0, 2) < 1).astype(jnp.int32), jax.random.fold_in(keys[4], 1), 0, 1),
        "layer_input": noise(keys[5], (BATCH, C, SITES), 1.0, 6.0, ((0, 8), (2, 4))),
        "pre_one": noise(keys[6], (BATCH, C, SITES), 1.0, 6.0, ((0, 8), (2, 4))),
        "pre_two": noise(keys[7], (BATCH, C, SITES), 1.0, 6.0, ((0, 8), (2, 4))),
        "conv_weight": noise(keys[8], (LAYERS, 9, C, C), (9 * C) ** -0.5, 0.125),
        "dilation": draw_dilation(jax.random.fold_in(keys[10], 71), 0),
    }


def reference(out_cot, mix_weight, corr_kernels, momentum, spin_up, layer_input, pre_one, pre_two, conv_weight, dilation):
    highest = lax.Precision.HIGHEST
    grad_rows = jnp.transpose(out_cot, (1, 0, 2)).reshape(C, BATCH * SITES)
    input_cot = jnp.dot(mix_weight.T, grad_rows, preferred_element_type=jnp.float32).reshape(C, BATCH, SIDE, SIDE)
    picked = jnp.transpose(corr_kernels[:, momentum], (0, 2, 1, 3))
    positions = jnp.arange(SIDE, dtype=jnp.int32)
    offsets = (positions[None, :] - positions[:, None]) % SIDE
    circ_rows = picked[0][:, :, offsets]
    circ_cols = picked[1][:, :, offsets]
    halfway = jnp.einsum('cbxX,cbxy->cbXy', circ_rows, input_cot, precision=highest)
    corr_grad = jnp.einsum('cbXy,cbyY->cbXY', halfway, circ_cols, precision=highest).astype(jnp.bfloat16)
    spin_gate = jnp.where(spin_up == 1, 1.5, 0.5).astype(jnp.float32).reshape(1, BATCH, SIDE, SIDE)
    grad_now = (corr_grad.astype(jnp.float32) * spin_gate).astype(jnp.bfloat16)
    norm_factor = 1.0 / math.sqrt(BATCH * SITES)
    layer_grads = [None] * LAYERS
    input_grad = None
    for conv_level in range(LAYERS - 1, -1, -1):
        slope_base = None
        if conv_level == 0:
            layer_values = jnp.transpose(layer_input, (1, 0, 2))
        else:
            saved_pre = pre_one if conv_level == 1 else pre_two
            slope_base = jnp.tanh(jnp.transpose(saved_pre, (1, 0, 2)).astype(jnp.float32))
            layer_values = slope_base.astype(jnp.bfloat16)
        value_rows = layer_values.reshape(C, BATCH * SITES)
        back_sum = jnp.zeros((C, BATCH * SITES), jnp.float32)
        tap_grads = []
        for row_step in (-1, 0, 1):
            for col_step in (-1, 0, 1):
                tap_index = (row_step + 1) * 3 + col_step + 1
                combined = jnp.roll(grad_now, (row_step, col_step), axis=(2, 3))
                for dilate in range(2, MAXDIL + 1):
                    shifted = jnp.roll(grad_now, (row_step * dilate, col_step * dilate), axis=(2, 3))
                    chosen_mask = (dilation[conv_level] == dilate)[:, None, None, None]
                    combined = jnp.where(chosen_mask, shifted, combined)
                combined_rows = combined.reshape(C, BATCH * SITES)
                back_sum = back_sum + jnp.dot(conv_weight[conv_level, tap_index].T, combined_rows, preferred_element_type=jnp.float32)
                tap_grads.append(jnp.dot(combined_rows, value_rows.T, preferred_element_type=jnp.float32) * norm_factor)
        layer_grads[conv_level] = jnp.stack(tap_grads)
        back_sum = back_sum.reshape(C, BATCH, SIDE, SIDE)
        if conv_level > 0:
            slope_grid = slope_base.reshape(C, BATCH, SIDE, SIDE)
            grad_now = (back_sum * (1.0 - slope_grid * slope_grid)).astype(jnp.bfloat16)
        else:
            input_grad = jnp.transpose(back_sum.reshape(C, BATCH, SITES), (1, 0, 2)).astype(jnp.bfloat16)
    return (input_grad, jnp.stack(layer_grads))
```

```python
import functools
import math

import jax
import jax.numpy as jnp
from jax import lax
from jax.experimental import pallas as pl
from jax.experimental.pallas import tpu as pltpu
from jax.sharding import PartitionSpec as P

SIDE = 64
LAYERS = 3
MAXDIL = 4
HALO = MAXDIL * SIDE
MESH = pl.DeviceIdType.MESH
VMEM = pl.BlockSpec(memory_space=pltpu.VMEM)
VMEM_LIMIT = 48 * 1024 * 1024


def enter(n):
    me = lax.axis_index("chan")
    barrier = pltpu.get_barrier_semaphore()
    for off in range(1, n):
        pl.semaphore_signal(
            barrier, inc=1, device_id={"chan": lax.rem(me + off, n)}, device_id_type=MESH
        )
    pl.semaphore_wait(barrier, n - 1)
    return me


def gather_kernel(n, x_ref, g_ref, xo_ref, go_ref, x_send, x_recv, g_send, g_recv, own):
    rows = x_ref.shape[0]
    me = enter(n)
    place = pl.ds(pl.multiple_of(me * rows, rows), rows)
    copies = []
    for off in range(1, n):
        peer = {"chan": lax.rem(me + off, n)}
        copies.append(
            pltpu.make_async_remote_copy(
                src_ref=x_ref, dst_ref=xo_ref.at[place],
                send_sem=x_send.at[off - 1], recv_sem=x_recv.at[off - 1],
                device_id=peer, device_id_type=MESH,
            )
        )
        copies.append(
            pltpu.make_async_remote_copy(
                src_ref=g_ref, dst_ref=go_ref.at[me],
                send_sem=g_send.at[off - 1], recv_sem=g_recv.at[off - 1],
                device_id=peer, device_id_type=MESH,
            )
        )
    copies.append(pltpu.make_async_copy(x_ref, xo_ref.at[place], own.at[0]))
    copies.append(pltpu.make_async_copy(g_ref, go_ref.at[me], own.at[1]))
    for copy in copies:
        copy.start()
    for copy in copies:
        copy.wait()


def gather(n, x, gate):
    rows, cells = x.shape
    return pl.pallas_call(
        functools.partial(gather_kernel, n),
        out_shape=(
            jax.ShapeDtypeStruct((n * rows, cells), x.dtype),
            jax.ShapeDtypeStruct((n,) + gate.shape, gate.dtype),
        ),
        in_specs=[VMEM, VMEM],
        out_specs=(VMEM, VMEM),
        scratch_shapes=[pltpu.SemaphoreType.DMA((n - 1,))] * 4 + [pltpu.SemaphoreType.DMA((2,))],
        compiler_params=pltpu.CompilerParams(
            collective_id=0, has_side_effects=True, vmem_limit_bytes=VMEM_LIMIT
        ),
        name="gather_blocks",
    )(x, gate)


def regroup_kernel(n, x_ref, o_ref, send, recv, own):
    rows, cells = x_ref.shape
    slab = cells // n
    me = enter(n)
    place = pl.ds(pl.multiple_of(me * rows, rows), rows)
    pieces = ((-HALO, 0, HALO), (0, HALO, slab), (slab, HALO + slab, HALO))
    copies = []
    for off in range(n):
        to = lax.rem(me + off, n)
        for piece, (shift, at, width) in enumerate(pieces):
            begin = pl.multiple_of(lax.rem(to * slab + shift + cells, cells), 128)
            src = x_ref.at[:, pl.ds(begin, width)]
            dst = o_ref.at[place, pl.ds(at, width)]
            if off == 0:
                copies.append(pltpu.make_async_copy(src, dst, own.at[piece]))
            else:
                copies.append(
                    pltpu.make_async_remote_copy(
                        src_ref=src, dst_ref=dst,
                        send_sem=send.at[off - 1, piece], recv_sem=recv.at[off - 1, piece],
                        device_id={"chan": to}, device_id_type=MESH,
                    )
                )
    for copy in copies[3:] + copies[:3]:
        copy.start()
    for copy in copies:
        copy.wait()


def regroup(n, x):
    rows, cells = x.shape
    return pl.pallas_call(
        functools.partial(regroup_kernel, n),
        out_shape=jax.ShapeDtypeStruct((n * rows, cells // n + 2 * HALO), x.dtype),
        in_specs=[VMEM],
        out_specs=VMEM,
        scratch_shapes=[pltpu.SemaphoreType.DMA((n - 1, 3))] * 2 + [pltpu.SemaphoreType.DMA((3,))],
        compiler_params=pltpu.CompilerParams(
            collective_id=1, has_side_effects=True, vmem_limit_bytes=VMEM_LIMIT
        ),
        name="regroup_rows",
    )(x)


def layer_kernel(level, norm, *refs):
    if level == LAYERS - 1:
        padded, dil, saved, weight, out, grads, col, taps = refs
    else:
        before, inner, after, dil, saved, weight, out, grads, col, taps = refs
    chans = weight.shape[1]
    cells = saved.shape[1]
    rows = cells // SIDE
    if level == LAYERS - 1:
        for start in range(0, cells + 2 * HALO, 256):
            block = padded[:, start : start + 256].astype(jnp.float32)
            col[1, start : start + 256, :] = block.T.astype(jnp.bfloat16)
    else:
        col[1, :HALO, :] = before[...]
        col[1, HALO : HALO + cells, :] = inner[...]
        col[1, HALO + cells :, :] = after[...]
    step = dil[...]

    def shift_columns(r, carry):
        at = pl.ds(pl.multiple_of(r * SIDE, SIDE), SIDE)
        value = col[1, at, :].astype(jnp.float32)
        for sign in (-1, 1):
            chosen = pltpu.roll(value, sign % SIDE, 0)
            for d in range(2, MAXDIL + 1):
                chosen = jnp.where(step == d, pltpu.roll(value, (sign * d) % SIDE, 0), chosen)
            col[sign + 1, at, :] = chosen.astype(jnp.bfloat16)
        return carry

    lax.fori_loop(0, rows + 2 * MAXDIL, shift_columns, 0)

    picks = [(step == d).astype(jnp.float32).astype(jnp.bfloat16) for d in range(1, MAXDIL + 1)]

    def shift_rows(r, carry):
        at = pl.ds(pl.multiple_of(r * SIDE, SIDE), SIDE)
        for i in (-1, 0, 1):
            for j in (-1, 0, 1):
                tap = 3 * (i + 1) + j + 1
                if i == 0:
                    value = col[j + 1, pl.ds(pl.multiple_of((r + MAXDIL) * SIDE, SIDE), SIDE), :]
                else:
                    value = None
                    for d in range(1, MAXDIL + 1):
                        begin = pl.multiple_of((r + MAXDIL - i * d) * SIDE, SIDE)
                        term = col[j + 1, pl.ds(begin, SIDE), :] * picks[d - 1]
                        value = term if value is None else value + term
                taps[at, tap * chans : (tap + 1) * chans] = value
        return carry

    lax.fori_loop(0, rows, shift_rows, 0)

    if level == 0:
        act = saved[...]
    else:
        act = jnp.tanh(saved[...].astype(jnp.float32)).astype(jnp.bfloat16)
    flat_weight = weight[...].reshape(9 * chans, chans)
    for start in range(0, cells, 256):
        back = jnp.dot(
            taps[start : start + 256, :], flat_weight, preferred_element_type=jnp.float32
        )
        if level == 0:
            out[:, start : start + 256] = back.T.astype(jnp.bfloat16)
        else:
            slope = jnp.tanh(saved[:, start : start + 256].astype(jnp.float32))
            slope = 1.0 - slope * slope
            out[start : start + 256, :] = (back * slope.T).astype(jnp.bfloat16)
    for tap in range(9):
        term = jnp.dot(
            act, taps[:, tap * chans : (tap + 1) * chans], preferred_element_type=jnp.float32
        )
        grads[tap] = (term * norm).T.astype(jnp.bfloat16)


def layer(level, norm, parts, dil, saved, weight):
    chans, cells = saved.shape
    out_dims = (chans, cells) if level == 0 else (cells, chans)
    flops = 2 * 2 * 9 * chans * chans * cells
    return pl.pallas_call(
        functools.partial(layer_kernel, level, norm),
        out_shape=(
            jax.ShapeDtypeStruct(out_dims, jnp.bfloat16),
            jax.ShapeDtypeStruct((9, chans, chans), jnp.bfloat16),
        ),
        in_specs=[VMEM] * (len(parts) + 3),
        out_specs=(VMEM, VMEM),
        scratch_shapes=[
            pltpu.VMEM((3, cells + 2 * HALO, chans), jnp.bfloat16),
            pltpu.VMEM((cells, 9 * chans), jnp.bfloat16),
        ],
        compiler_params=pltpu.CompilerParams(vmem_limit_bytes=VMEM_LIMIT),
        cost_estimate=pl.CostEstimate(
            flops=flops, bytes_accessed=8 * 1024 * 1024, transcendentals=chans * cells
        ),
        name="conv_backward",
    )(*parts, dil, saved, weight)


def on_device(
    out_cot,
    mix_weight,
    corr_kernels,
    momentum,
    spin_up,
    layer_input,
    pre_one,
    pre_two,
    conv_weight,
    dilation,
):
    chan_block = out_cot.shape[1]
    site_count = out_cot.shape[2]
    side = corr_kernels.shape[3]
    n = lax.axis_size("chan")
    slab = layer_input.shape[2]
    own_start = lax.axis_index("chan") * chan_block
    gate = jnp.where(spin_up == 1, 1.5, 0.5).astype(jnp.float32)
    gate = jnp.broadcast_to(gate, (8, slab))
    everything, gates = gather(n, out_cot[0], gate)
    gates = gates[:, 0, :].reshape(1, side, side)
    own_columns = lax.dynamic_slice_in_dim(mix_weight, own_start, chan_block, 1)
    input_cot = jnp.einsum(
        "oc,on->cn", own_columns, everything, preferred_element_type=jnp.float32
    )
    picked = lax.dynamic_index_in_dim(corr_kernels, momentum[0], axis=1, keepdims=False)
    positions = jnp.arange(side, dtype=jnp.int32)
    circ_table = (
        (positions[None, :] - positions[:, None]) % side == positions[:, None, None]
    ).astype(jnp.float32)
    circulant = jnp.einsum(
        "aci,ixy->acxy", picked, circ_table, precision=lax.Precision.HIGHEST
    )
    grid_values = input_cot.reshape(chan_block, side, side)
    high = lax.Precision.HIGH
    halfway = jnp.einsum("cxX,cxy->cXy", circulant[0], grid_values, precision=high)
    corr_grad = jnp.einsum("cXy,cyY->cXY", halfway, circulant[1], precision=high)
    corr_grad = corr_grad.astype(jnp.bfloat16).astype(jnp.float32)
    gated = (corr_grad * gates).astype(jnp.bfloat16).reshape(chan_block, site_count)
    padded = regroup(n, gated)
    norm = 1.0 / math.sqrt(out_cot.shape[0] * lax.axis_size("samp") * site_count)
    up = [(i, (i + 1) % n) for i in range(n)]
    down = [(j, i) for i, j in up]
    saved = (layer_input[0], pre_one[0], pre_two[0])
    layer_grads = [None] * LAYERS
    parts = (padded,)
    result = None
    for level in range(LAYERS - 1, -1, -1):
        result, local_grad = layer(
            level, norm, parts, dilation[level][None, :], saved[level], conv_weight[level]
        )
        reduced = lax.psum_scatter(local_grad, "chan", scatter_dimension=1, tiled=True)
        layer_grads[level] = lax.psum(reduced, "samp").astype(jnp.float32)
        if level > 0:
            before = lax.ppermute(result[slab - HALO :], "chan", up)
            after = lax.ppermute(result[:HALO], "chan", down)
            parts = (before, result, after)
    return (result[None], jnp.stack(layer_grads))


def solution(mesh):
    in_specs = (
        P("samp", "chan", None),
        P(),
        P(None, None, "chan", None),
        P("samp"),
        P("samp", "chan"),
        P("samp", None, "chan"),
        P("samp", None, "chan"),
        P("samp", None, "chan"),
        P(),
        P(),
    )
    out_specs = (P("samp", None, "chan"), P(None, None, "chan", None))
    return jax.shard_map(
        on_device, mesh=mesh, in_specs=in_specs, out_specs=out_specs, check_vma=False
    )
```

```python
import functools
import math

import jax
import jax.numpy as jnp
from jax import lax
from jax.experimental import pallas as pl
from jax.experimental.pallas import tpu as pltpu
from jax.sharding import PartitionSpec as P

SIDE = 64
LAYERS = 3
MAXDIL = 4
HALO = MAXDIL * SIDE
MESH = pl.DeviceIdType.MESH
VMEM = pl.BlockSpec(memory_space=pltpu.VMEM)
VMEM_LIMIT = 48 * 1024 * 1024


def enter(n):
    me = lax.axis_index("chan")
    barrier = pltpu.get_barrier_semaphore()
    for off in range(1, n):
        pl.semaphore_signal(
            barrier, inc=1, device_id={"chan": lax.rem(me + off, n)}, device_id_type=MESH
        )
    pl.semaphore_wait(barrier, n - 1)
    return me


def gather_kernel(n, x_ref, g_ref, xo_ref, go_ref, x_send, x_recv, g_send, g_recv, own):
    rows = x_ref.shape[0]
    me = enter(n)
    place = pl.ds(pl.multiple_of(me * rows, rows), rows)
    copies = []
    for off in range(1, n):
        peer = {"chan": lax.rem(me + off, n)}
        copies.append(
            pltpu.make_async_remote_copy(
                src_ref=x_ref, dst_ref=xo_ref.at[place],
                send_sem=x_send.at[off - 1], recv_sem=x_recv.at[off - 1],
                device_id=peer, device_id_type=MESH,
            )
        )
        copies.append(
            pltpu.make_async_remote_copy(
                src_ref=g_ref, dst_ref=go_ref.at[me],
                send_sem=g_send.at[off - 1], recv_sem=g_recv.at[off - 1],
                device_id=peer, device_id_type=MESH,
            )
        )
    copies.append(pltpu.make_async_copy(x_ref, xo_ref.at[place], own.at[0]))
    copies.append(pltpu.make_async_copy(g_ref, go_ref.at[me], own.at[1]))
    for copy in copies:
        copy.start()
    for copy in copies:
        copy.wait()


def gather(n, x, gate):
    rows, cells = x.shape
    return pl.pallas_call(
        functools.partial(gather_kernel, n),
        out_shape=(
            jax.ShapeDtypeStruct((n * rows, cells), x.dtype),
            jax.ShapeDtypeStruct((n,) + gate.shape, gate.dtype),
        ),
        in_specs=[VMEM, VMEM],
        out_specs=(VMEM, VMEM),
        scratch_shapes=[pltpu.SemaphoreType.DMA((n - 1,))] * 4 + [pltpu.SemaphoreType.DMA((2,))],
        compiler_params=pltpu.CompilerParams(
            collective_id=0, has_side_effects=True, vmem_limit_bytes=VMEM_LIMIT
        ),
        name="gather_blocks",
    )(x, gate)


def regroup_kernel(n, x_ref, o_ref, send, recv, own):
    rows, cells = x_ref.shape
    slab = cells // n
    me = enter(n)
    place = pl.ds(pl.multiple_of(me * rows, rows), rows)
    pieces = ((-HALO, 0, HALO), (0, HALO, slab), (slab, HALO + slab, HALO))
    copies = []
    for off in range(n):
        to = lax.rem(me + off, n)
        for piece, (shift, at, width) in enumerate(pieces):
            begin = pl.multiple_of(lax.rem(to * slab + shift + cells, cells), 128)
            src = x_ref.at[:, pl.ds(begin, width)]
            dst = o_ref.at[place, pl.ds(at, width)]
            if off == 0:
                copies.append(pltpu.make_async_copy(src, dst, own.at[piece]))
            else:
                copies.append(
                    pltpu.make_async_remote_copy(
                        src_ref=src, dst_ref=dst,
                        send_sem=send.at[off - 1, piece], recv_sem=recv.at[off - 1, piece],
                        device_id={"chan": to}, device_id_type=MESH,
                    )
                )
    for copy in copies[3:] + copies[:3]:
        copy.start()
    for copy in copies:
        copy.wait()


def regroup(n, x):
    rows, cells = x.shape
    return pl.pallas_call(
        functools.partial(regroup_kernel, n),
        out_shape=jax.ShapeDtypeStruct((n * rows, cells // n + 2 * HALO), x.dtype),
        in_specs=[VMEM],
        out_specs=VMEM,
        scratch_shapes=[pltpu.SemaphoreType.DMA((n - 1, 3))] * 2 + [pltpu.SemaphoreType.DMA((3,))],
        compiler_params=pltpu.CompilerParams(
            collective_id=1, has_side_effects=True, vmem_limit_bytes=VMEM_LIMIT
        ),
        name="regroup_rows",
    )(x)


def layer_kernel(level, norm, *refs):
    if level == LAYERS - 1:
        padded, dil, saved, weight, out, grads, col, taps = refs
    else:
        before, inner, after, dil, saved, weight, out, grads, col, taps = refs
    chans = weight.shape[1]
    cells = saved.shape[1]
    rows = cells // SIDE
    if level == LAYERS - 1:
        for start in range(0, cells + 2 * HALO, 256):
            block = padded[:, start : start + 256].astype(jnp.float32)
            col[1, start : start + 256, :] = block.T.astype(jnp.bfloat16)
    else:
        col[1, :HALO, :] = before[...]
        col[1, HALO : HALO + cells, :] = inner[...]
        col[1, HALO + cells :, :] = after[...]
    step = dil[...]

    def shift_columns(r, carry):
        at = pl.ds(pl.multiple_of(r * SIDE, SIDE), SIDE)
        value = col[1, at, :].astype(jnp.float32)
        for sign in (-1, 1):
            chosen = pltpu.roll(value, sign % SIDE, 0)
            for d in range(2, MAXDIL + 1):
                chosen = jnp.where(step == d, pltpu.roll(value, (sign * d) % SIDE, 0), chosen)
            col[sign + 1, at, :] = chosen.astype(jnp.bfloat16)
        return carry

    lax.fori_loop(0, rows + 2 * MAXDIL, shift_columns, 0)

    picks = [(step == d).astype(jnp.float32).astype(jnp.bfloat16) for d in range(1, MAXDIL + 1)]

    def shift_rows(r, carry):
        at = pl.ds(pl.multiple_of(r * SIDE, SIDE), SIDE)
        for i in (-1, 0, 1):
            for j in (-1, 0, 1):
                tap = 3 * (i + 1) + j + 1
                if i == 0:
                    value = col[j + 1, pl.ds(pl.multiple_of((r + MAXDIL) * SIDE, SIDE), SIDE), :]
                else:
                    value = None
                    for d in range(1, MAXDIL + 1):
                        begin = pl.multiple_of((r + MAXDIL - i * d) * SIDE, SIDE)
                        term = col[j + 1, pl.ds(begin, SIDE), :] * picks[d - 1]
                        value = term if value is None else value + term
                taps[at, tap * chans : (tap + 1) * chans] = value
        return carry

    lax.fori_loop(0, rows, shift_rows, 0)

    if level == 0:
        act = saved[...]
    else:
        act = jnp.tanh(saved[...].astype(jnp.float32)).astype(jnp.bfloat16)
    flat_weight = weight[...].reshape(9 * chans, chans)
    for start in range(0, cells, 256):
        back = jnp.dot(
            taps[start : start + 256, :], flat_weight, preferred_element_type=jnp.float32
        )
        if level == 0:
            out[:, start : start + 256] = back.T.astype(jnp.bfloat16)
        else:
            slope = jnp.tanh(saved[:, start : start + 256].astype(jnp.float32))
            slope = 1.0 - slope * slope
            out[start : start + 256, :] = (back * slope.T).astype(jnp.bfloat16)
    for tap in range(9):
        term = jnp.dot(
            act, taps[:, tap * chans : (tap + 1) * chans], preferred_element_type=jnp.float32
        )
        grads[tap] = (term * norm).T.astype(jnp.bfloat16)


def layer(level, norm, parts, dil, saved, weight):
    chans, cells = saved.shape
    out_dims = (chans, cells) if level == 0 else (cells, chans)
    flops = 2 * 2 * 9 * chans * chans * cells
    return pl.pallas_call(
        functools.partial(layer_kernel, level, norm),
        out_shape=(
            jax.ShapeDtypeStruct(out_dims, jnp.bfloat16),
            jax.ShapeDtypeStruct((9, chans, chans), jnp.bfloat16),
        ),
        in_specs=[VMEM] * (len(parts) + 3),
        out_specs=(VMEM, VMEM),
        scratch_shapes=[
            pltpu.VMEM((3, cells + 2 * HALO, chans), jnp.bfloat16),
            pltpu.VMEM((cells, 9 * chans), jnp.bfloat16),
        ],
        compiler_params=pltpu.CompilerParams(vmem_limit_bytes=VMEM_LIMIT),
        cost_estimate=pl.CostEstimate(
            flops=flops, bytes_accessed=8 * 1024 * 1024, transcendentals=chans * cells
        ),
        name="conv_backward",
    )(*parts, dil, saved, weight)


def reduce_kernel(m, nz, *refs):
    parts, out = refs[:LAYERS], refs[LAYERS]
    pair_in, pair_sum, chan_in, chan_sum, z_in, z_sum, full = refs[LAYERS + 1 : LAYERS + 8]
    sems = refs[LAYERS + 8 :]
    taps, _, width = pair_in.shape[1:]
    block, share = chan_sum.shape[2], z_sum.shape[1]
    me = lax.axis_index("chan")
    samp = lax.axis_index("samp")
    core, z = lax.rem(samp, 2), lax.div(samp, 2)
    pair = {"samp": 2 * z + 1 - core}
    chans = [lax.rem(me + off, m) for off in range(1, m)]
    zs = [lax.rem(z + off, nz) for off in range(1, nz)]
    barrier = pltpu.get_barrier_semaphore()
    peers = [pair] + [{"chan": c} for c in chans] + [{"samp": 2 * k + core} for k in zs]
    for peer in peers:
        pl.semaphore_signal(barrier, inc=1, device_id=peer, device_id_type=MESH)
    pl.semaphore_wait(barrier, len(peers))

    def send(src, dst, sem, place, peer):
        copy = pltpu.make_async_remote_copy(
            src_ref=src, dst_ref=dst, send_sem=sem[0].at[place], recv_sem=sem[1].at[place],
            device_id=peer, device_id_type=MESH,
        )
        copy.start()
        return copy

    def lanes(k):
        return pl.ds(pl.multiple_of(k * width, width), width)

    def rows(k):
        return pl.ds(pl.multiple_of(k * block, block), block)

    f32 = jnp.float32
    order = range(LAYERS - 1, -1, -1)
    sent = []
    stage = {}
    for l in order:
        stage[l] = [
            send(parts[l].at[:, :, lanes(1 - core)], pair_in.at[l], sems[0:2], l, pair)
        ]
        sent += stage[l]
    for l in order:
        for copy in stage[l]:
            copy.wait_recv()

        def add_pair(t, carry, l=l):
            total = parts[l][t, :, lanes(core)].astype(f32) + pair_in[l, t].astype(f32)
            pair_sum[l, t] = total.astype(jnp.bfloat16)
            return carry

        lax.fori_loop(0, taps, add_pair, 0)
        stage[l] = [
            send(
                pair_sum.at[l, :, rows(c), :], chan_in.at[l, off], sems[2:4], (l, off),
                {"chan": c},
            )
            for off, c in enumerate(chans)
        ]
        sent += stage[l]
    for l in order:
        for copy in stage[l]:
            copy.wait_recv()

        def add_chan(t, carry, l=l):
            total = pair_sum[l, t, rows(me), :].astype(f32)
            for off in range(m - 1):
                total = total + chan_in[l, off, t].astype(f32)
            chan_sum[l, t] = total.astype(jnp.bfloat16)
            return carry

        lax.fori_loop(0, taps, add_chan, 0)
        for t in range(taps, nz * share):
            chan_sum[l, t] = jnp.zeros((block, width), jnp.bfloat16)
        stage[l] = [
            send(
                chan_sum.at[l, pl.ds(k * share, share)], z_in.at[l, off], sems[4:6], (l, off),
                {"samp": 2 * k + core},
            )
            for off, k in enumerate(zs)
        ]
        sent += stage[l]
    for l in order:
        for copy in stage[l]:
            copy.wait_recv()
        for t in range(share):
            total = chan_sum[l, z * share + t].astype(f32)
            for off in range(nz - 1):
                total = total + z_in[l, off, t].astype(f32)
            z_sum[l, t] = total.astype(jnp.bfloat16)
            full[l, core, z * share + t] = total.astype(jnp.bfloat16)
        place = pl.ds(z * share, share)
        stage[l] = [
            send(
                z_sum.at[l], full.at[l, core, place], sems[6:8], (l, off),
                {"samp": 2 * k + core},
            )
            for off, k in enumerate(zs)
        ]
        sent += stage[l]
    for l in order:
        for copy in stage[l]:
            copy.wait_recv()
        stage[l] = [send(full.at[l, core], full.at[l, core], sems[8:10], l, pair)]
        sent += stage[l]
    for l in order:
        for copy in stage[l]:
            copy.wait_recv()

        def widen(t, carry, l=l):
            for k in range(2):
                out[l, t, :, k * width : (k + 1) * width] = full[l, k, t].astype(f32)
            return carry

        lax.fori_loop(0, taps, widen, 0)
    for copy in sent:
        copy.wait_send()


def reduce_grads(m, samples, grads):
    taps, chans, width = grads[0].shape
    nz, half, block = samples // 2, width // 2, chans // m
    share = -(-taps // nz)
    dma, bf16 = pltpu.SemaphoreType.DMA, jnp.bfloat16
    return pl.pallas_call(
        functools.partial(reduce_kernel, m, nz),
        out_shape=jax.ShapeDtypeStruct((LAYERS, taps, block, width), jnp.float32),
        in_specs=[VMEM] * LAYERS,
        out_specs=VMEM,
        scratch_shapes=[
            pltpu.VMEM((LAYERS, taps, chans, half), bf16),
            pltpu.VMEM((LAYERS, taps, chans, half), bf16),
            pltpu.VMEM((LAYERS, m - 1, taps, block, half), bf16),
            pltpu.VMEM((LAYERS, nz * share, block, half), bf16),
            pltpu.VMEM((LAYERS, nz - 1, share, block, half), bf16),
            pltpu.VMEM((LAYERS, share, block, half), bf16),
            pltpu.VMEM((LAYERS, 2, nz * share, block, half), bf16),
            dma((LAYERS,)), dma((LAYERS,)),
            dma((LAYERS, m - 1)), dma((LAYERS, m - 1)),
            dma((LAYERS, nz - 1)), dma((LAYERS, nz - 1)),
            dma((LAYERS, nz - 1)), dma((LAYERS, nz - 1)),
            dma((LAYERS,)), dma((LAYERS,)),
        ],
        compiler_params=pltpu.CompilerParams(
            collective_id=2, has_side_effects=True, vmem_limit_bytes=VMEM_LIMIT
        ),
        name="reduce_grads",
    )(*grads)


def on_device(
    out_cot,
    mix_weight,
    corr_kernels,
    momentum,
    spin_up,
    layer_input,
    pre_one,
    pre_two,
    conv_weight,
    dilation,
):
    chan_block = out_cot.shape[1]
    site_count = out_cot.shape[2]
    side = corr_kernels.shape[3]
    n = lax.axis_size("chan")
    slab = layer_input.shape[2]
    own_start = lax.axis_index("chan") * chan_block
    gate = jnp.where(spin_up == 1, 1.5, 0.5).astype(jnp.float32)
    gate = jnp.broadcast_to(gate, (8, slab))
    everything, gates = gather(n, out_cot[0], gate)
    gates = gates[:, 0, :].reshape(1, side, side)
    own_columns = lax.dynamic_slice_in_dim(mix_weight, own_start, chan_block, 1)
    input_cot = jnp.einsum(
        "oc,on->cn", own_columns, everything, preferred_element_type=jnp.float32
    )
    picked = lax.dynamic_index_in_dim(corr_kernels, momentum[0], axis=1, keepdims=False)
    positions = jnp.arange(side, dtype=jnp.int32)
    circ_table = (
        (positions[None, :] - positions[:, None]) % side == positions[:, None, None]
    ).astype(jnp.float32)
    circulant = jnp.einsum(
        "aci,ixy->acxy", picked, circ_table, precision=lax.Precision.HIGHEST
    )
    grid_values = input_cot.reshape(chan_block, side, side)
    high = lax.Precision.HIGH
    halfway = jnp.einsum("cxX,cxy->cXy", circulant[0], grid_values, precision=high)
    corr_grad = jnp.einsum("cXy,cyY->cXY", halfway, circulant[1], precision=high)
    corr_grad = corr_grad.astype(jnp.bfloat16).astype(jnp.float32)
    gated = (corr_grad * gates).astype(jnp.bfloat16).reshape(chan_block, site_count)
    padded = regroup(n, gated)
    norm = 1.0 / math.sqrt(out_cot.shape[0] * lax.axis_size("samp") * site_count)
    up = [(i, (i + 1) % n) for i in range(n)]
    down = [(j, i) for i, j in up]
    saved = (layer_input[0], pre_one[0], pre_two[0])
    layer_grads = [None] * LAYERS
    parts = (padded,)
    result = None
    for level in range(LAYERS - 1, -1, -1):
        result, local_grad = layer(
            level, norm, parts, dilation[level][None, :], saved[level], conv_weight[level]
        )
        layer_grads[level] = local_grad
        if level > 0:
            before = lax.ppermute(result[slab - HALO :], "chan", up)
            after = lax.ppermute(result[:HALO], "chan", down)
            parts = (before, result, after)
    weight_grad = reduce_grads(n, lax.axis_size("samp"), layer_grads)
    return (result[None], weight_grad)


def solution(mesh):
    in_specs = (
        P("samp", "chan", None),
        P(),
        P(None, None, "chan", None),
        P("samp"),
        P("samp", "chan"),
        P("samp", None, "chan"),
        P("samp", None, "chan"),
        P("samp", None, "chan"),
        P(),
        P(),
    )
    out_specs = (P("samp", None, "chan"), P(None, None, "chan", None))
    return jax.shard_map(
        on_device, mesh=mesh, in_specs=in_specs, out_specs=out_specs, check_vma=False
    )
```

```python
import functools
import math

import jax
import jax.numpy as jnp
from jax import lax
from jax.experimental import pallas as pl
from jax.experimental.pallas import tpu as pltpu
from jax.sharding import PartitionSpec as P

SIDE = 64
LAYERS = 3
MAXDIL = 4
HALO = MAXDIL * SIDE
MESH = pl.DeviceIdType.MESH
VMEM = pl.BlockSpec(memory_space=pltpu.VMEM)
VMEM_LIMIT = 48 * 1024 * 1024


def enter(n):
    me = lax.axis_index("chan")
    barrier = pltpu.get_barrier_semaphore()
    for off in range(1, n):
        pl.semaphore_signal(
            barrier, inc=1, device_id={"chan": lax.rem(me + off, n)}, device_id_type=MESH
        )
    pl.semaphore_wait(barrier, n - 1)
    return me


def gather_kernel(n, x_ref, g_ref, xo_ref, go_ref, x_send, x_recv, g_send, g_recv, own):
    rows = x_ref.shape[0]
    me = enter(n)
    place = pl.ds(pl.multiple_of(me * rows, rows), rows)
    copies = []
    for off in range(1, n):
        peer = {"chan": lax.rem(me + off, n)}
        copies.append(
            pltpu.make_async_remote_copy(
                src_ref=x_ref, dst_ref=xo_ref.at[place],
                send_sem=x_send.at[off - 1], recv_sem=x_recv.at[off - 1],
                device_id=peer, device_id_type=MESH,
            )
        )
        copies.append(
            pltpu.make_async_remote_copy(
                src_ref=g_ref, dst_ref=go_ref.at[me],
                send_sem=g_send.at[off - 1], recv_sem=g_recv.at[off - 1],
                device_id=peer, device_id_type=MESH,
            )
        )
    copies.append(pltpu.make_async_copy(x_ref, xo_ref.at[place], own.at[0]))
    copies.append(pltpu.make_async_copy(g_ref, go_ref.at[me], own.at[1]))
    for copy in copies:
        copy.start()
    for copy in copies:
        copy.wait()


def gather(n, x, gate):
    rows, cells = x.shape
    return pl.pallas_call(
        functools.partial(gather_kernel, n),
        out_shape=(
            jax.ShapeDtypeStruct((n * rows, cells), x.dtype),
            jax.ShapeDtypeStruct((n,) + gate.shape, gate.dtype),
        ),
        in_specs=[VMEM, VMEM],
        out_specs=(VMEM, VMEM),
        scratch_shapes=[pltpu.SemaphoreType.DMA((n - 1,))] * 4 + [pltpu.SemaphoreType.DMA((2,))],
        compiler_params=pltpu.CompilerParams(
            collective_id=0, has_side_effects=True, vmem_limit_bytes=VMEM_LIMIT
        ),
        name="gather_blocks",
    )(x, gate)


def regroup_kernel(n, x_ref, o_ref, send, recv, own):
    rows, cells = x_ref.shape
    slab = cells // n
    me = enter(n)
    place = pl.ds(pl.multiple_of(me * rows, rows), rows)
    pieces = ((-HALO, 0, HALO), (0, HALO, slab), (slab, HALO + slab, HALO))
    copies = []
    for off in range(n):
        to = lax.rem(me + off, n)
        for piece, (shift, at, width) in enumerate(pieces):
            begin = pl.multiple_of(lax.rem(to * slab + shift + cells, cells), 128)
            src = x_ref.at[:, pl.ds(begin, width)]
            dst = o_ref.at[place, pl.ds(at, width)]
            if off == 0:
                copies.append(pltpu.make_async_copy(src, dst, own.at[piece]))
            else:
                copies.append(
                    pltpu.make_async_remote_copy(
                        src_ref=src, dst_ref=dst,
                        send_sem=send.at[off - 1, piece], recv_sem=recv.at[off - 1, piece],
                        device_id={"chan": to}, device_id_type=MESH,
                    )
                )
    for copy in copies[3:] + copies[:3]:
        copy.start()
    for copy in copies:
        copy.wait()


def regroup(n, x):
    rows, cells = x.shape
    return pl.pallas_call(
        functools.partial(regroup_kernel, n),
        out_shape=jax.ShapeDtypeStruct((n * rows, cells // n + 2 * HALO), x.dtype),
        in_specs=[VMEM],
        out_specs=VMEM,
        scratch_shapes=[pltpu.SemaphoreType.DMA((n - 1, 3))] * 2 + [pltpu.SemaphoreType.DMA((3,))],
        compiler_params=pltpu.CompilerParams(
            collective_id=1, has_side_effects=True, vmem_limit_bytes=VMEM_LIMIT
        ),
        name="regroup_rows",
    )(x)


def backward_kernel(m, nz, norm, *refs):
    padded, dil, weight = refs[:3]
    saved, (out, summed) = refs[3 : 3 + LAYERS], refs[3 + LAYERS : 5 + LAYERS]
    rest = refs[5 + LAYERS :]
    col, taps, halo, grads = rest[:4]
    pair_in, pair_sum, chan_in, chan_sum, z_in, z_sum, full = rest[4:11]
    sems = rest[11:]
    f32, bf16 = jnp.float32, jnp.bfloat16
    tap_count, _, width = pair_in.shape[1:]
    block, share = chan_sum.shape[2], z_sum.shape[1]
    chans, cells = weight.shape[2], saved[0].shape[1]
    side_rows = cells // SIDE
    me = lax.axis_index("chan")
    samp = lax.axis_index("samp")
    core, z = lax.rem(samp, 2), lax.div(samp, 2)
    pair = {"samp": 2 * z + 1 - core}
    others = [lax.rem(me + off, m) for off in range(1, m)]
    zs = [lax.rem(z + off, nz) for off in range(1, nz)]
    barrier = pltpu.get_barrier_semaphore()
    peers = [pair] + [{"chan": c} for c in others] + [{"samp": 2 * k + core} for k in zs]
    for peer in peers:
        pl.semaphore_signal(barrier, inc=1, device_id=peer, device_id_type=MESH)
    pl.semaphore_wait(barrier, len(peers))

    def send(src, dst, sem, place, peer):
        copy = pltpu.make_async_remote_copy(
            src_ref=src, dst_ref=dst, send_sem=sem[0].at[place], recv_sem=sem[1].at[place],
            device_id=peer, device_id_type=MESH,
        )
        copy.start()
        return copy

    def lanes(k):
        return pl.ds(pl.multiple_of(k * width, width), width)

    def rows(k):
        return pl.ds(pl.multiple_of(k * block, block), block)

    stage = [[] for _ in range(LAYERS)]
    sent = []

    def arrived(l):
        for copy in stage[l]:
            copy.wait_recv()

    def go(l, copies):
        stage[l] = copies
        sent.extend(copies)

    def start_pair(l):
        src = grads.at[l, :, :, lanes(1 - core)]
        go(l, [send(src, pair_in.at[l], sems[0:2], l, pair)])

    def pair_to_chan(l):
        arrived(l)

        def add_pair(t, carry):
            total = grads[l, t, :, lanes(core)].astype(f32) + pair_in[l, t].astype(f32)
            pair_sum[l, t] = total.astype(bf16)
            return carry

        lax.fori_loop(0, tap_count, add_pair, 0)
        go(l, [
            send(
                pair_sum.at[l, :, rows(c), :], chan_in.at[l, off], sems[2:4], (l, off),
                {"chan": c},
            )
            for off, c in enumerate(others)
        ])

    def chan_to_z(l):
        arrived(l)

        def add_chan(t, carry):
            total = pair_sum[l, t, rows(me), :].astype(f32)
            for off in range(m - 1):
                total = total + chan_in[l, off, t].astype(f32)
            chan_sum[l, t] = total.astype(bf16)
            return carry

        lax.fori_loop(0, tap_count, add_chan, 0)
        for t in range(tap_count, nz * share):
            chan_sum[l, t] = jnp.zeros((block, width), bf16)
        go(l, [
            send(
                chan_sum.at[l, pl.ds(k * share, share)], z_in.at[l, off], sems[4:6], (l, off),
                {"samp": 2 * k + core},
            )
            for off, k in enumerate(zs)
        ])

    def z_to_full(l):
        arrived(l)
        for t in range(share):
            total = chan_sum[l, z * share + t].astype(f32)
            for off in range(nz - 1):
                total = total + z_in[l, off, t].astype(f32)
            z_sum[l, t] = total.astype(bf16)
            full[l, core, z * share + t] = total.astype(bf16)
        place = pl.ds(z * share, share)
        go(l, [
            send(z_sum.at[l], full.at[l, core, place], sems[6:8], (l, off), {"samp": 2 * k + core})
            for off, k in enumerate(zs)
        ])

    def full_to_pair(l):
        arrived(l)
        go(l, [send(full.at[l, core], full.at[l, core], sems[8:10], l, pair)])

    def finish(l):
        arrived(l)

        def widen(t, carry):
            for k in range(2):
                summed[l, t, :, k * width : (k + 1) * width] = full[l, k, t].astype(f32)
            return carry

        lax.fori_loop(0, tap_count, widen, 0)

    edge = []
    for level in range(LAYERS - 1, -1, -1):
        if level == LAYERS - 1:
            for start in range(0, cells + 2 * HALO, 256):
                piece = padded[:, start : start + 256].astype(f32)
                col[1, start : start + 256, :] = piece.T.astype(bf16)
        else:
            for copy in edge:
                copy.wait()
            col[1, :HALO, :] = halo[level, 0]
            col[1, HALO + cells :, :] = halo[level, 1]
        step = dil[level : level + 1, :]

        def shift_columns(r, carry, step=step):
            at = pl.ds(pl.multiple_of(r * SIDE, SIDE), SIDE)
            value = col[1, at, :].astype(f32)
            for sign in (-1, 1):
                chosen = pltpu.roll(value, sign % SIDE, 0)
                for d in range(2, MAXDIL + 1):
                    chosen = jnp.where(step == d, pltpu.roll(value, (sign * d) % SIDE, 0), chosen)
                col[sign + 1, at, :] = chosen.astype(bf16)
            return carry

        lax.fori_loop(0, side_rows + 2 * MAXDIL, shift_columns, 0)
        if level < LAYERS - 1:
            pair_to_chan(level + 1)
        picks = [(step == d).astype(f32).astype(bf16) for d in range(1, MAXDIL + 1)]

        def shift_rows(r, carry, picks=picks):
            at = pl.ds(pl.multiple_of(r * SIDE, SIDE), SIDE)
            for i in (-1, 0, 1):
                for j in (-1, 0, 1):
                    tap = 3 * (i + 1) + j + 1
                    if i == 0:
                        begin = pl.multiple_of((r + MAXDIL) * SIDE, SIDE)
                        value = col[j + 1, pl.ds(begin, SIDE), :]
                    else:
                        value = None
                        for d in range(1, MAXDIL + 1):
                            begin = pl.multiple_of((r + MAXDIL - i * d) * SIDE, SIDE)
                            term = col[j + 1, pl.ds(begin, SIDE), :] * picks[d - 1]
                            value = term if value is None else value + term
                    taps[at, tap * chans : (tap + 1) * chans] = value
            return carry

        lax.fori_loop(0, side_rows, shift_rows, 0)
        flat_weight = weight[level].reshape(tap_count * chans, chans)
        for start in range(0, cells, 256):
            back = jnp.dot(taps[start : start + 256, :], flat_weight, preferred_element_type=f32)
            if level == 0:
                out[:, start : start + 256] = back.T.astype(bf16)
            else:
                slope = jnp.tanh(saved[level][:, start : start + 256].astype(f32))
                slope = 1.0 - slope * slope
                col[1, HALO + start : HALO + start + 256, :] = (back * slope.T).astype(bf16)
        if level > 0:
            up, down = {"chan": others[0]}, {"chan": others[m - 2]}
            edge = [
                send(
                    col.at[1, pl.ds(cells, HALO), :], halo.at[level - 1, 0],
                    sems[10:12], (level - 1, 0), up,
                ),
                send(
                    col.at[1, pl.ds(HALO, HALO), :], halo.at[level - 1, 1],
                    sems[10:12], (level - 1, 1), down,
                ),
            ]
            act = jnp.tanh(saved[level][...].astype(f32)).astype(bf16)
        else:
            chan_to_z(LAYERS - 1)
            act = saved[level][...]
        for tap in range(tap_count):
            term = jnp.dot(
                act, taps[:, tap * chans : (tap + 1) * chans], preferred_element_type=f32
            )
            grads[level, tap] = (term * norm).T.astype(bf16)
        start_pair(level)
    z_to_full(2)
    pair_to_chan(0)
    full_to_pair(2)
    chan_to_z(1)
    z_to_full(1)
    finish(2)
    chan_to_z(0)
    full_to_pair(1)
    z_to_full(0)
    finish(1)
    full_to_pair(0)
    finish(0)
    for copy in sent:
        copy.wait_send()


def backward(m, samples, norm, padded, dil, weight, saved):
    chans, cells = saved[0].shape
    nz, half, block, taps = samples // 2, chans // 2, chans // m, weight.shape[1]
    share = -(-taps // nz)
    dma, bf16 = pltpu.SemaphoreType.DMA, jnp.bfloat16
    return pl.pallas_call(
        functools.partial(backward_kernel, m, nz, norm),
        out_shape=(
            jax.ShapeDtypeStruct((chans, cells), bf16),
            jax.ShapeDtypeStruct((LAYERS, taps, block, chans), jnp.float32),
        ),
        in_specs=[VMEM] * (3 + LAYERS),
        out_specs=(VMEM, VMEM),
        scratch_shapes=[
            pltpu.VMEM((3, cells + 2 * HALO, chans), bf16),
            pltpu.VMEM((cells, taps * chans), bf16),
            pltpu.VMEM((LAYERS - 1, 2, HALO, chans), bf16),
            pltpu.VMEM((LAYERS, taps, chans, chans), bf16),
            pltpu.VMEM((LAYERS, taps, chans, half), bf16),
            pltpu.VMEM((LAYERS, taps, chans, half), bf16),
            pltpu.VMEM((LAYERS, m - 1, taps, block, half), bf16),
            pltpu.VMEM((LAYERS, nz * share, block, half), bf16),
            pltpu.VMEM((LAYERS, nz - 1, share, block, half), bf16),
            pltpu.VMEM((LAYERS, share, block, half), bf16),
            pltpu.VMEM((LAYERS, 2, nz * share, block, half), bf16),
            dma((LAYERS,)), dma((LAYERS,)),
            dma((LAYERS, m - 1)), dma((LAYERS, m - 1)),
            dma((LAYERS, nz - 1)), dma((LAYERS, nz - 1)),
            dma((LAYERS, nz - 1)), dma((LAYERS, nz - 1)),
            dma((LAYERS,)), dma((LAYERS,)),
            dma((LAYERS - 1, 2)), dma((LAYERS - 1, 2)),
        ],
        compiler_params=pltpu.CompilerParams(
            collective_id=2, has_side_effects=True, vmem_limit_bytes=VMEM_LIMIT
        ),
        name="conv_backward",
    )(padded, dil, weight, *saved)


def on_device(
    out_cot,
    mix_weight,
    corr_kernels,
    momentum,
    spin_up,
    layer_input,
    pre_one,
    pre_two,
    conv_weight,
    dilation,
):
    chan_block = out_cot.shape[1]
    site_count = out_cot.shape[2]
    side = corr_kernels.shape[3]
    n = lax.axis_size("chan")
    slab = layer_input.shape[2]
    own_start = lax.axis_index("chan") * chan_block
    gate = jnp.where(spin_up == 1, 1.5, 0.5).astype(jnp.float32)
    gate = jnp.broadcast_to(gate, (8, slab))
    everything, gates = gather(n, out_cot[0], gate)
    gates = gates[:, 0, :].reshape(1, side, side)
    own_columns = lax.dynamic_slice_in_dim(mix_weight, own_start, chan_block, 1)
    input_cot = jnp.einsum(
        "oc,on->cn", own_columns, everything, preferred_element_type=jnp.float32
    )
    picked = lax.dynamic_index_in_dim(corr_kernels, momentum[0], axis=1, keepdims=False)
    positions = jnp.arange(side, dtype=jnp.int32)
    circ_table = (
        (positions[None, :] - positions[:, None]) % side == positions[:, None, None]
    ).astype(jnp.float32)
    circulant = jnp.einsum(
        "aci,ixy->acxy", picked, circ_table, precision=lax.Precision.HIGHEST
    )
    grid_values = input_cot.reshape(chan_block, side, side)
    high = lax.Precision.HIGH
    halfway = jnp.einsum("cxX,cxy->cXy", circulant[0], grid_values, precision=high)
    corr_grad = jnp.einsum("cXy,cyY->cXY", halfway, circulant[1], precision=high)
    corr_grad = corr_grad.astype(jnp.bfloat16).astype(jnp.float32)
    gated = (corr_grad * gates).astype(jnp.bfloat16).reshape(chan_block, site_count)
    padded = regroup(n, gated)
    norm = 1.0 / math.sqrt(out_cot.shape[0] * lax.axis_size("samp") * site_count)
    saved = (layer_input[0], pre_one[0], pre_two[0])
    result, weight_grad = backward(
        n, lax.axis_size("samp"), norm, padded, dilation, conv_weight, saved
    )
    return (result[None], weight_grad)


def solution(mesh):
    in_specs = (
        P("samp", "chan", None),
        P(),
        P(None, None, "chan", None),
        P("samp"),
        P("samp", "chan"),
        P("samp", None, "chan"),
        P("samp", None, "chan"),
        P("samp", None, "chan"),
        P(),
        P(),
    )
    out_specs = (P("samp", None, "chan"), P(None, None, "chan", None))
    return jax.shard_map(
        on_device, mesh=mesh, in_specs=in_specs, out_specs=out_specs, check_vma=False
    )
```

```python
import functools
import math

import jax
import jax.numpy as jnp
from jax import lax
from jax.experimental import pallas as pl
from jax.experimental.pallas import tpu as pltpu
from jax.sharding import PartitionSpec as P

SIDE = 64
LAYERS = 3
MAXDIL = 4
HALO = MAXDIL * SIDE
MESH = pl.DeviceIdType.MESH
VMEM = pl.BlockSpec(memory_space=pltpu.VMEM)
VMEM_LIMIT = 34 * 1024 * 1024


def enter(n):
    me = lax.axis_index("chan")
    barrier = pltpu.get_barrier_semaphore()
    for off in range(1, n):
        pl.semaphore_signal(
            barrier, inc=1, device_id={"chan": lax.rem(me + off, n)}, device_id_type=MESH
        )
    pl.semaphore_wait(barrier, n - 1)
    return me


def mix_kernel(n, x_ref, g_ref, w_ref, o_ref, go_ref, sites, mixed, *sems):
    rows, cells = x_ref.shape
    slab = cells // n
    me = enter(n)
    own_rows = pl.ds(pl.multiple_of(me * rows, rows), rows)
    own_cells = pl.ds(pl.multiple_of(me * slab, slab), slab)

    def move(src, dst, place, off, to):
        if off == 0:
            copy = pltpu.make_async_copy(src, dst, sems[2 * place + 1].at[n - 1])
        else:
            copy = pltpu.make_async_remote_copy(
                src_ref=src, dst_ref=dst,
                send_sem=sems[2 * place].at[off - 1], recv_sem=sems[2 * place + 1].at[off - 1],
                device_id={"chan": to}, device_id_type=MESH,
            )
        copy.start()
        return copy

    turns = [(off, lax.rem(me + off, n)) for off in list(range(1, n)) + [0]]
    copies = [
        move(
            x_ref.at[:, pl.ds(pl.multiple_of(to * slab, slab), slab)],
            sites.at[own_rows], 0, off, to,
        )
        for off, to in turns
    ]
    gates = [move(g_ref, go_ref.at[me], 1, off, to) for off, to in turns]
    for copy in copies:
        copy.wait()
    for start in range(0, slab, 256):
        part = jnp.dot(
            w_ref[...], sites[:, start : start + 256], preferred_element_type=jnp.float32
        )
        mixed[:, start : start + 256] = part.astype(jnp.bfloat16)
    copies = [
        move(
            mixed.at[pl.ds(pl.multiple_of(to * rows, rows), rows)],
            o_ref.at[:, own_cells], 2, off, to,
        )
        for off, to in turns
    ]
    for copy in gates + copies:
        copy.wait()


def mix(n, x, gate, weight):
    rows, cells = x.shape
    return pl.pallas_call(
        functools.partial(mix_kernel, n),
        out_shape=(
            jax.ShapeDtypeStruct((rows, cells), jnp.bfloat16),
            jax.ShapeDtypeStruct((n,) + gate.shape, gate.dtype),
        ),
        in_specs=[VMEM] * 3,
        out_specs=(VMEM, VMEM),
        scratch_shapes=[
            pltpu.VMEM((n * rows, cells // n), jnp.bfloat16),
            pltpu.VMEM((n * rows, cells // n), jnp.bfloat16),
        ]
        + [pltpu.SemaphoreType.DMA((n,))] * 6,
        compiler_params=pltpu.CompilerParams(
            collective_id=0, has_side_effects=True, vmem_limit_bytes=12 * 1024 * 1024
        ),
        name="mix_channels",
    )(x, gate, weight)


def regroup_kernel(n, x_ref, o_ref, send, recv, own):
    rows, cells = x_ref.shape
    slab = cells // n
    me = enter(n)
    place = pl.ds(pl.multiple_of(me * rows, rows), rows)
    pieces = ((-HALO, 0, HALO), (0, HALO, slab), (slab, HALO + slab, HALO))
    copies = []
    for off in range(n):
        to = lax.rem(me + off, n)
        for piece, (shift, at, width) in enumerate(pieces):
            begin = pl.multiple_of(lax.rem(to * slab + shift + cells, cells), 128)
            src = x_ref.at[:, pl.ds(begin, width)]
            dst = o_ref.at[place, pl.ds(at, width)]
            if off == 0:
                copies.append(pltpu.make_async_copy(src, dst, own.at[piece]))
            else:
                copies.append(
                    pltpu.make_async_remote_copy(
                        src_ref=src, dst_ref=dst,
                        send_sem=send.at[off - 1, piece], recv_sem=recv.at[off - 1, piece],
                        device_id={"chan": to}, device_id_type=MESH,
                    )
                )
    for copy in copies[3:] + copies[:3]:
        copy.start()
    for copy in copies:
        copy.wait()


def regroup(n, x):
    rows, cells = x.shape
    return pl.pallas_call(
        functools.partial(regroup_kernel, n),
        out_shape=jax.ShapeDtypeStruct((n * rows, cells // n + 2 * HALO), x.dtype),
        in_specs=[VMEM],
        out_specs=VMEM,
        scratch_shapes=[pltpu.SemaphoreType.DMA((n - 1, 3))] * 2 + [pltpu.SemaphoreType.DMA((3,))],
        compiler_params=pltpu.CompilerParams(
            collective_id=1, has_side_effects=True, vmem_limit_bytes=8 * 1024 * 1024
        ),
        name="regroup_rows",
    )(x)


def backward_kernel(m, nz, norm, *refs):
    padded, dil, weight = refs[:3]
    saved, (out, summed) = refs[3 : 3 + LAYERS], refs[3 + LAYERS : 5 + LAYERS]
    rest = refs[5 + LAYERS :]
    col, taps, halo, grads = rest[:4]
    pair_in, pair_sum, chan_in, chan_sum, z_in, z_sum, full = rest[4:11]
    sems = rest[11:]
    f32, bf16 = jnp.float32, jnp.bfloat16
    tap_count, _, width = pair_in.shape[1:]
    block, share = chan_sum.shape[2], z_sum.shape[1]
    chans, cells = weight.shape[2], saved[0].shape[1]
    side_rows = cells // SIDE
    me = lax.axis_index("chan")
    samp = lax.axis_index("samp")
    core, z = lax.rem(samp, 2), lax.div(samp, 2)
    pair = {"samp": 2 * z + 1 - core}
    others = [lax.rem(me + off, m) for off in range(1, m)]
    zs = [lax.rem(z + off, nz) for off in range(1, nz)]
    barrier = pltpu.get_barrier_semaphore()
    peers = [pair] + [{"chan": c} for c in others] + [{"samp": 2 * k + core} for k in zs]
    for peer in peers:
        pl.semaphore_signal(barrier, inc=1, device_id=peer, device_id_type=MESH)
    pl.semaphore_wait(barrier, len(peers))

    def send(src, dst, sem, place, peer):
        copy = pltpu.make_async_remote_copy(
            src_ref=src, dst_ref=dst, send_sem=sem[0].at[place], recv_sem=sem[1].at[place],
            device_id=peer, device_id_type=MESH,
        )
        copy.start()
        return copy

    def lanes(k):
        return pl.ds(pl.multiple_of(k * width, width), width)

    def rows(k):
        return pl.ds(pl.multiple_of(k * block, block), block)

    stage = [[] for _ in range(LAYERS)]
    sent = []

    def arrived(l):
        for copy in stage[l]:
            copy.wait_recv()

    def go(l, copies):
        stage[l] = copies
        sent.extend(copies)

    def start_pair(l):
        src = grads.at[l, :, :, lanes(1 - core)]
        go(l, [send(src, pair_in.at[l], sems[0:2], l, pair)])

    def pair_to_chan(l):
        arrived(l)

        def add_pair(t, carry):
            total = grads[l, t, :, lanes(core)].astype(f32) + pair_in[l, t].astype(f32)
            pair_sum[l, t] = total.astype(bf16)
            return carry

        lax.fori_loop(0, tap_count, add_pair, 0)
        go(l, [
            send(
                pair_sum.at[l, :, rows(c), :], chan_in.at[l, off], sems[2:4], (l, off),
                {"chan": c},
            )
            for off, c in enumerate(others)
        ])

    def chan_to_z(l):
        arrived(l)

        def add_chan(t, carry):
            total = pair_sum[l, t, rows(me), :].astype(f32)
            for off in range(m - 1):
                total = total + chan_in[l, off, t].astype(f32)
            chan_sum[l, t] = total.astype(bf16)
            return carry

        lax.fori_loop(0, tap_count, add_chan, 0)
        for t in range(tap_count, nz * share):
            chan_sum[l, t] = jnp.zeros((block, width), bf16)
        go(l, [
            send(
                chan_sum.at[l, pl.ds(k * share, share)], z_in.at[l, off], sems[4:6], (l, off),
                {"samp": 2 * k + core},
            )
            for off, k in enumerate(zs)
        ])

    def z_to_full(l):
        arrived(l)
        for t in range(share):
            total = chan_sum[l, z * share + t].astype(f32)
            for off in range(nz - 1):
                total = total + z_in[l, off, t].astype(f32)
            z_sum[l, t] = total.astype(bf16)
            full[l, core, z * share + t] = total.astype(bf16)
        place = pl.ds(z * share, share)
        go(l, [
            send(z_sum.at[l], full.at[l, core, place], sems[6:8], (l, off), {"samp": 2 * k + core})
            for off, k in enumerate(zs)
        ])

    def full_to_pair(l):
        arrived(l)
        go(l, [send(full.at[l, core], full.at[l, core], sems[8:10], l, pair)])

    def finish(l):
        arrived(l)

        def widen(t, carry):
            for k in range(2):
                summed[l, t, :, k * width : (k + 1) * width] = full[l, k, t].astype(f32)
            return carry

        lax.fori_loop(0, tap_count, widen, 0)

    edge = []
    for level in range(LAYERS - 1, -1, -1):
        if level == LAYERS - 1:
            for start in range(0, cells + 2 * HALO, 256):
                piece = padded[:, start : start + 256].astype(f32)
                col[1, start : start + 256, :] = piece.T.astype(bf16)
        else:
            for copy in edge:
                copy.wait()
            col[1, :HALO, :] = halo[level, 0]
            col[1, HALO + cells :, :] = halo[level, 1]
        step = dil[level : level + 1, :]

        def shift_columns(r, carry, step=step):
            at = pl.ds(pl.multiple_of(r * SIDE, SIDE), SIDE)
            value = col[1, at, :].astype(f32)
            for sign in (-1, 1):
                chosen = pltpu.roll(value, sign % SIDE, 0)
                for d in range(2, MAXDIL + 1):
                    chosen = jnp.where(step == d, pltpu.roll(value, (sign * d) % SIDE, 0), chosen)
                col[sign + 1, at, :] = chosen.astype(bf16)
            return carry

        lax.fori_loop(0, side_rows + 2 * MAXDIL, shift_columns, 0)
        if level < LAYERS - 1:
            pair_to_chan(level + 1)
        picks = [(step == d).astype(f32).astype(bf16) for d in range(1, MAXDIL + 1)]

        def shift_rows(r, carry, picks=picks):
            at = pl.ds(pl.multiple_of(r * SIDE, SIDE), SIDE)
            for i in (-1, 0, 1):
                for j in (-1, 0, 1):
                    tap = 3 * (i + 1) + j + 1
                    if i == 0:
                        begin = pl.multiple_of((r + MAXDIL) * SIDE, SIDE)
                        value = col[j + 1, pl.ds(begin, SIDE), :]
                    else:
                        value = None
                        for d in range(1, MAXDIL + 1):
                            begin = pl.multiple_of((r + MAXDIL - i * d) * SIDE, SIDE)
                            term = col[j + 1, pl.ds(begin, SIDE), :] * picks[d - 1]
                            value = term if value is None else value + term
                    taps[at, tap * chans : (tap + 1) * chans] = value
            return carry

        lax.fori_loop(0, side_rows, shift_rows, 0)
        flat_weight = weight[level].reshape(tap_count * chans, chans)
        for start in range(0, cells, 256):
            back = jnp.dot(taps[start : start + 256, :], flat_weight, preferred_element_type=f32)
            if level == 0:
                out[:, start : start + 256] = back.T.astype(bf16)
            else:
                slope = jnp.tanh(saved[level][:, start : start + 256].astype(f32))
                slope = 1.0 - slope * slope
                col[1, HALO + start : HALO + start + 256, :] = (back * slope.T).astype(bf16)
        if level > 0:
            up, down = {"chan": others[0]}, {"chan": others[m - 2]}
            edge = [
                send(
                    col.at[1, pl.ds(cells, HALO), :], halo.at[level - 1, 0],
                    sems[10:12], (level - 1, 0), up,
                ),
                send(
                    col.at[1, pl.ds(HALO, HALO), :], halo.at[level - 1, 1],
                    sems[10:12], (level - 1, 1), down,
                ),
            ]
            act = jnp.tanh(saved[level][...].astype(f32)).astype(bf16)
        else:
            chan_to_z(LAYERS - 1)
            act = saved[level][...]
        for tap in range(tap_count):
            term = jnp.dot(
                act, taps[:, tap * chans : (tap + 1) * chans], preferred_element_type=f32
            )
            grads[level, tap] = (term * norm).T.astype(bf16)
        start_pair(level)
    z_to_full(2)
    pair_to_chan(0)
    full_to_pair(2)
    chan_to_z(1)
    z_to_full(1)
    finish(2)
    chan_to_z(0)
    full_to_pair(1)
    z_to_full(0)
    finish(1)
    full_to_pair(0)
    finish(0)
    for copy in sent:
        copy.wait_send()


def backward(m, samples, norm, padded, dil, weight, saved):
    chans, cells = saved[0].shape
    nz, half, block, taps = samples // 2, chans // 2, chans // m, weight.shape[1]
    share = -(-taps // nz)
    dma, bf16 = pltpu.SemaphoreType.DMA, jnp.bfloat16
    return pl.pallas_call(
        functools.partial(backward_kernel, m, nz, norm),
        out_shape=(
            jax.ShapeDtypeStruct((chans, cells), bf16),
            jax.ShapeDtypeStruct((LAYERS, taps, block, chans), jnp.float32),
        ),
        in_specs=[VMEM] * (3 + LAYERS),
        out_specs=(VMEM, VMEM),
        scratch_shapes=[
            pltpu.VMEM((3, cells + 2 * HALO, chans), bf16),
            pltpu.VMEM((cells, taps * chans), bf16),
            pltpu.VMEM((LAYERS - 1, 2, HALO, chans), bf16),
            pltpu.VMEM((LAYERS, taps, chans, chans), bf16),
            pltpu.VMEM((LAYERS, taps, chans, half), bf16),
            pltpu.VMEM((LAYERS, taps, chans, half), bf16),
            pltpu.VMEM((LAYERS, m - 1, taps, block, half), bf16),
            pltpu.VMEM((LAYERS, nz * share, block, half), bf16),
            pltpu.VMEM((LAYERS, nz - 1, share, block, half), bf16),
            pltpu.VMEM((LAYERS, share, block, half), bf16),
            pltpu.VMEM((LAYERS, 2, nz * share, block, half), bf16),
            dma((LAYERS,)), dma((LAYERS,)),
            dma((LAYERS, m - 1)), dma((LAYERS, m - 1)),
            dma((LAYERS, nz - 1)), dma((LAYERS, nz - 1)),
            dma((LAYERS, nz - 1)), dma((LAYERS, nz - 1)),
            dma((LAYERS,)), dma((LAYERS,)),
            dma((LAYERS - 1, 2)), dma((LAYERS - 1, 2)),
        ],
        compiler_params=pltpu.CompilerParams(
            collective_id=2, has_side_effects=True, vmem_limit_bytes=VMEM_LIMIT
        ),
        name="conv_backward",
    )(padded, dil, weight, *saved)


def on_device(
    out_cot,
    mix_weight,
    corr_kernels,
    momentum,
    spin_up,
    layer_input,
    pre_one,
    pre_two,
    conv_weight,
    dilation,
):
    chan_block = out_cot.shape[1]
    site_count = out_cot.shape[2]
    side = corr_kernels.shape[3]
    n = lax.axis_size("chan")
    slab = layer_input.shape[2]
    gate = jnp.where(spin_up == 1, 1.5, 0.5).astype(jnp.float32)
    gate = jnp.broadcast_to(gate, (8, slab))
    input_cot, gates = mix(n, out_cot[0], gate, mix_weight.T)
    gates = gates[:, 0, :].reshape(1, side, side)
    picked = lax.dynamic_index_in_dim(corr_kernels, momentum[0], axis=1, keepdims=False)
    positions = jnp.arange(side, dtype=jnp.int32)
    circ_table = (
        (positions[None, :] - positions[:, None]) % side == positions[:, None, None]
    ).astype(jnp.float32)
    circulant = jnp.einsum(
        "aci,ixy->acxy", picked, circ_table, precision=lax.Precision.HIGHEST
    )
    grid_values = input_cot.astype(jnp.float32).reshape(chan_block, side, side)
    high = lax.Precision.HIGH
    halfway = jnp.einsum("cxX,cxy->cXy", circulant[0], grid_values, precision=high)
    corr_grad = jnp.einsum("cXy,cyY->cXY", halfway, circulant[1], precision=high)
    corr_grad = corr_grad.astype(jnp.bfloat16).astype(jnp.float32)
    gated = (corr_grad * gates).astype(jnp.bfloat16).reshape(chan_block, site_count)
    padded = regroup(n, gated)
    norm = 1.0 / math.sqrt(out_cot.shape[0] * lax.axis_size("samp") * site_count)
    saved = (layer_input[0], pre_one[0], pre_two[0])
    result, weight_grad = backward(
        n, lax.axis_size("samp"), norm, padded, dilation, conv_weight, saved
    )
    return (result[None], weight_grad)


def solution(mesh):
    in_specs = (
        P("samp", "chan", None),
        P(),
        P(None, None, "chan", None),
        P("samp"),
        P("samp", "chan"),
        P("samp", None, "chan"),
        P("samp", None, "chan"),
        P("samp", None, "chan"),
        P(),
        P(),
    )
    out_specs = (P("samp", None, "chan"), P(None, None, "chan", None))
    return jax.shard_map(
        on_device, mesh=mesh, in_specs=in_specs, out_specs=out_specs, check_vma=False
    )
```

```python
import functools
import math

import jax
import jax.numpy as jnp
from jax import lax
from jax.experimental import pallas as pl
from jax.experimental.pallas import tpu as pltpu
from jax.sharding import PartitionSpec as P

SIDE = 64
LAYERS = 3
MAXDIL = 4
HALO = MAXDIL * SIDE
MESH = pl.DeviceIdType.MESH
VMEM = pl.BlockSpec(memory_space=pltpu.VMEM)
VMEM_LIMIT = 34 * 1024 * 1024


def enter(n):
    me = lax.axis_index("chan")
    barrier = pltpu.get_barrier_semaphore()
    for off in range(1, n):
        pl.semaphore_signal(
            barrier, inc=1, device_id={"chan": lax.rem(me + off, n)}, device_id_type=MESH
        )
    pl.semaphore_wait(barrier, n - 1)
    return me


def mix_kernel(n, x_ref, g_ref, w_ref, o_ref, go_ref, sites, mixed, *sems):
    rows, cells = x_ref.shape
    slab = cells // n
    me = enter(n)
    own_rows = pl.ds(pl.multiple_of(me * rows, rows), rows)
    own_cells = pl.ds(pl.multiple_of(me * slab, slab), slab)

    def move(src, dst, place, off, to):
        if off == 0:
            copy = pltpu.make_async_copy(src, dst, sems[2 * place + 1].at[n - 1])
        else:
            copy = pltpu.make_async_remote_copy(
                src_ref=src, dst_ref=dst,
                send_sem=sems[2 * place].at[off - 1], recv_sem=sems[2 * place + 1].at[off - 1],
                device_id={"chan": to}, device_id_type=MESH,
            )
        copy.start()
        return copy

    turns = [(off, lax.rem(me + off, n)) for off in list(range(1, n)) + [0]]
    copies = [
        move(
            x_ref.at[:, pl.ds(pl.multiple_of(to * slab, slab), slab)],
            sites.at[own_rows], 0, off, to,
        )
        for off, to in turns
    ]
    gates = [move(g_ref, go_ref.at[me], 1, off, to) for off, to in turns]
    for copy in copies:
        copy.wait()
    for start in range(0, slab, 256):
        part = jnp.dot(
            w_ref[...], sites[:, start : start + 256], preferred_element_type=jnp.float32
        )
        mixed[:, start : start + 256] = part.astype(jnp.bfloat16)
    copies = [
        move(
            mixed.at[pl.ds(pl.multiple_of(to * rows, rows), rows)],
            o_ref.at[:, own_cells], 2, off, to,
        )
        for off, to in turns
    ]
    for copy in gates + copies:
        copy.wait()


def mix(n, x, gate, weight):
    rows, cells = x.shape
    return pl.pallas_call(
        functools.partial(mix_kernel, n),
        out_shape=(
            jax.ShapeDtypeStruct((rows, cells), jnp.bfloat16),
            jax.ShapeDtypeStruct((n,) + gate.shape, gate.dtype),
        ),
        in_specs=[VMEM] * 3,
        out_specs=(VMEM, VMEM),
        scratch_shapes=[
            pltpu.VMEM((n * rows, cells // n), jnp.bfloat16),
            pltpu.VMEM((n * rows, cells // n), jnp.bfloat16),
        ]
        + [pltpu.SemaphoreType.DMA((n,))] * 6,
        compiler_params=pltpu.CompilerParams(
            collective_id=0, has_side_effects=True, vmem_limit_bytes=12 * 1024 * 1024
        ),
        name="mix_channels",
    )(x, gate, weight)


def regroup_kernel(n, x_ref, o_ref, send, recv, own):
    rows, cells = x_ref.shape
    slab = cells // n
    me = enter(n)
    place = pl.ds(pl.multiple_of(me * rows, rows), rows)
    pieces = ((-HALO, 0, HALO), (0, HALO, slab), (slab, HALO + slab, HALO))
    copies = []
    for off in range(n):
        to = lax.rem(me + off, n)
        for piece, (shift, at, width) in enumerate(pieces):
            begin = pl.multiple_of(lax.rem(to * slab + shift + cells, cells), 128)
            src = x_ref.at[:, pl.ds(begin, width)]
            dst = o_ref.at[place, pl.ds(at, width)]
            if off == 0:
                copies.append(pltpu.make_async_copy(src, dst, own.at[piece]))
            else:
                copies.append(
                    pltpu.make_async_remote_copy(
                        src_ref=src, dst_ref=dst,
                        send_sem=send.at[off - 1, piece], recv_sem=recv.at[off - 1, piece],
                        device_id={"chan": to}, device_id_type=MESH,
                    )
                )
    for copy in copies[3:] + copies[:3]:
        copy.start()
    for copy in copies:
        copy.wait()


def regroup(n, x):
    rows, cells = x.shape
    return pl.pallas_call(
        functools.partial(regroup_kernel, n),
        out_shape=jax.ShapeDtypeStruct((n * rows, cells // n + 2 * HALO), x.dtype),
        in_specs=[VMEM],
        out_specs=VMEM,
        scratch_shapes=[pltpu.SemaphoreType.DMA((n - 1, 3))] * 2 + [pltpu.SemaphoreType.DMA((3,))],
        compiler_params=pltpu.CompilerParams(
            collective_id=1, has_side_effects=True, vmem_limit_bytes=8 * 1024 * 1024
        ),
        name="regroup_rows",
    )(x)


def backward_kernel(m, nz, norm, *refs):
    padded, dil, weight = refs[:3]
    saved, (out, summed) = refs[3 : 3 + LAYERS], refs[3 + LAYERS : 5 + LAYERS]
    rest = refs[5 + LAYERS :]
    col, taps, halo, grads = rest[:4]
    pair_in, pair_sum, chan_in, chan_sum, z_in, z_sum, full = rest[4:11]
    sems = rest[11:]
    f32, bf16 = jnp.float32, jnp.bfloat16
    tap_count, _, width = pair_in.shape[1:]
    block, share = chan_sum.shape[2], z_sum.shape[1]
    chans, cells = weight.shape[2], saved[0].shape[1]
    side_rows = cells // SIDE
    me = lax.axis_index("chan")
    samp = lax.axis_index("samp")
    core, z = lax.rem(samp, 2), lax.div(samp, 2)
    pair = {"samp": 2 * z + 1 - core}
    others = [lax.rem(me + off, m) for off in range(1, m)]
    zs = [lax.rem(z + off, nz) for off in range(1, nz)]
    barrier = pltpu.get_barrier_semaphore()
    peers = [pair] + [{"chan": c} for c in others] + [{"samp": 2 * k + core} for k in zs]
    for peer in peers:
        pl.semaphore_signal(barrier, inc=1, device_id=peer, device_id_type=MESH)
    pl.semaphore_wait(barrier, len(peers))

    def send(src, dst, sem, place, peer):
        copy = pltpu.make_async_remote_copy(
            src_ref=src, dst_ref=dst, send_sem=sem[0].at[place], recv_sem=sem[1].at[place],
            device_id=peer, device_id_type=MESH,
        )
        copy.start()
        return copy

    def lanes(k):
        return pl.ds(pl.multiple_of(k * width, width), width)

    def rows(k):
        return pl.ds(pl.multiple_of(k * block, block), block)

    stage = [[] for _ in range(LAYERS)]
    sent = []

    def arrived(l):
        for copy in stage[l]:
            copy.wait_recv()

    def go(l, copies):
        stage[l] = copies
        sent.extend(copies)

    def start_pair(l):
        src = grads.at[l, :, :, lanes(1 - core)]
        go(l, [send(src, pair_in.at[l], sems[0:2], l, pair)])

    def pair_to_chan(l):
        arrived(l)

        def add_pair(t, carry):
            total = grads[l, t, :, lanes(core)].astype(f32) + pair_in[l, t].astype(f32)
            pair_sum[l, t] = total.astype(bf16)
            return carry

        lax.fori_loop(0, tap_count, add_pair, 0)
        go(l, [
            send(
                pair_sum.at[l, :, rows(c), :], chan_in.at[l, off], sems[2:4], (l, off),
                {"chan": c},
            )
            for off, c in enumerate(others)
        ])

    def chan_to_z(l):
        arrived(l)

        def add_chan(t, carry):
            total = pair_sum[l, t, rows(me), :].astype(f32)
            for off in range(m - 1):
                total = total + chan_in[l, off, t].astype(f32)
            chan_sum[l, t] = total.astype(bf16)
            return carry

        lax.fori_loop(0, tap_count, add_chan, 0)
        for t in range(tap_count, nz * share):
            chan_sum[l, t] = jnp.zeros((block, width), bf16)
        go(l, [
            send(
                chan_sum.at[l, pl.ds(k * share, share)], z_in.at[l, off], sems[4:6], (l, off),
                {"samp": 2 * k + core},
            )
            for off, k in enumerate(zs)
        ])

    def z_to_full(l):
        arrived(l)
        for t in range(share):
            total = chan_sum[l, z * share + t].astype(f32)
            for off in range(nz - 1):
                total = total + z_in[l, off, t].astype(f32)
            z_sum[l, t] = total.astype(bf16)
            full[l, core, z * share + t] = total.astype(bf16)
        place = pl.ds(z * share, share)
        go(l, [
            send(z_sum.at[l], full.at[l, core, place], sems[6:8], (l, off), {"samp": 2 * k + core})
            for off, k in enumerate(zs)
        ])

    def full_to_pair(l):
        arrived(l)
        go(l, [send(full.at[l, core], full.at[l, core], sems[8:10], l, pair)])

    def finish(l):
        arrived(l)

        def widen(t, carry):
            for k in range(2):
                summed[l, t, :, k * width : (k + 1) * width] = full[l, k, t].astype(f32)
            return carry

        lax.fori_loop(0, tap_count, widen, 0)

    edge = []
    for level in range(LAYERS - 1, -1, -1):
        if level == LAYERS - 1:
            for start in range(0, cells + 2 * HALO, 256):
                piece = padded[:, start : start + 256].astype(f32)
                col[1, start : start + 256, :] = piece.T.astype(bf16)
        else:
            for copy in edge:
                copy.wait()
            col[1, :HALO, :] = halo[level, 0]
            col[1, HALO + cells :, :] = halo[level, 1]
        step = dil[level : level + 1, :]

        def shift_columns(r, carry, step=step):
            at = pl.ds(pl.multiple_of(r * SIDE, SIDE), SIDE)
            value = col[1, at, :].astype(f32)
            for sign in (-1, 1):
                chosen = pltpu.roll(value, sign % SIDE, 0)
                for d in range(2, MAXDIL + 1):
                    chosen = jnp.where(step == d, pltpu.roll(value, (sign * d) % SIDE, 0), chosen)
                col[sign + 1, at, :] = chosen.astype(bf16)
            return carry

        lax.fori_loop(0, side_rows + 2 * MAXDIL, shift_columns, 0)
        if level == 0:
            pair_to_chan(1)
        picks = [(step == d).astype(f32).astype(bf16) for d in range(1, MAXDIL + 1)]

        def shift_rows(r, carry, picks=picks):
            at = pl.ds(pl.multiple_of(r * SIDE, SIDE), SIDE)
            for i in (-1, 0, 1):
                for j in (-1, 0, 1):
                    tap = 3 * (i + 1) + j + 1
                    if i == 0:
                        begin = pl.multiple_of((r + MAXDIL) * SIDE, SIDE)
                        value = col[j + 1, pl.ds(begin, SIDE), :]
                    else:
                        value = None
                        for d in range(1, MAXDIL + 1):
                            begin = pl.multiple_of((r + MAXDIL - i * d) * SIDE, SIDE)
                            term = col[j + 1, pl.ds(begin, SIDE), :] * picks[d - 1]
                            value = term if value is None else value + term
                    taps[at, tap * chans : (tap + 1) * chans] = value
            return carry

        lax.fori_loop(0, side_rows, shift_rows, 0)
        flat_weight = weight[level].reshape(tap_count * chans, chans)
        for start in range(0, cells, 256):
            back = jnp.dot(taps[start : start + 256, :], flat_weight, preferred_element_type=f32)
            if level == 0:
                out[:, start : start + 256] = back.T.astype(bf16)
            else:
                slope = jnp.tanh(saved[level][:, start : start + 256].astype(f32))
                slope = 1.0 - slope * slope
                col[1, HALO + start : HALO + start + 256, :] = (back * slope.T).astype(bf16)
        if level > 0:
            up, down = {"chan": others[0]}, {"chan": others[m - 2]}
            edge = [
                send(
                    col.at[1, pl.ds(cells, HALO), :], halo.at[level - 1, 0],
                    sems[10:12], (level - 1, 0), up,
                ),
                send(
                    col.at[1, pl.ds(HALO, HALO), :], halo.at[level - 1, 1],
                    sems[10:12], (level - 1, 1), down,
                ),
            ]
            if level < LAYERS - 1:
                pair_to_chan(level + 1)
            act = jnp.tanh(saved[level][...].astype(f32)).astype(bf16)
        else:
            chan_to_z(LAYERS - 1)
            act = saved[level][...]
        for tap in range(tap_count):
            term = jnp.dot(
                act, taps[:, tap * chans : (tap + 1) * chans], preferred_element_type=f32
            )
            grads[level, tap] = (term * norm).T.astype(bf16)
        start_pair(level)
    z_to_full(2)
    pair_to_chan(0)
    full_to_pair(2)
    chan_to_z(1)
    z_to_full(1)
    finish(2)
    chan_to_z(0)
    full_to_pair(1)
    z_to_full(0)
    finish(1)
    full_to_pair(0)
    finish(0)
    for copy in sent:
        copy.wait_send()


def backward(m, samples, norm, padded, dil, weight, saved):
    chans, cells = saved[0].shape
    nz, half, block, taps = samples // 2, chans // 2, chans // m, weight.shape[1]
    share = -(-taps // nz)
    dma, bf16 = pltpu.SemaphoreType.DMA, jnp.bfloat16
    return pl.pallas_call(
        functools.partial(backward_kernel, m, nz, norm),
        out_shape=(
            jax.ShapeDtypeStruct((chans, cells), bf16),
            jax.ShapeDtypeStruct((LAYERS, taps, block, chans), jnp.float32),
        ),
        in_specs=[VMEM] * (3 + LAYERS),
        out_specs=(VMEM, VMEM),
        scratch_shapes=[
            pltpu.VMEM((3, cells + 2 * HALO, chans), bf16),
            pltpu.VMEM((cells, taps * chans), bf16),
            pltpu.VMEM((LAYERS - 1, 2, HALO, chans), bf16),
            pltpu.VMEM((LAYERS, taps, chans, chans), bf16),
            pltpu.VMEM((LAYERS, taps, chans, half), bf16),
            pltpu.VMEM((LAYERS, taps, chans, half), bf16),
            pltpu.VMEM((LAYERS, m - 1, taps, block, half), bf16),
            pltpu.VMEM((LAYERS, nz * share, block, half), bf16),
            pltpu.VMEM((LAYERS, nz - 1, share, block, half), bf16),
            pltpu.VMEM((LAYERS, share, block, half), bf16),
            pltpu.VMEM((LAYERS, 2, nz * share, block, half), bf16),
            dma((LAYERS,)), dma((LAYERS,)),
            dma((LAYERS, m - 1)), dma((LAYERS, m - 1)),
            dma((LAYERS, nz - 1)), dma((LAYERS, nz - 1)),
            dma((LAYERS, nz - 1)), dma((LAYERS, nz - 1)),
            dma((LAYERS,)), dma((LAYERS,)),
            dma((LAYERS - 1, 2)), dma((LAYERS - 1, 2)),
        ],
        compiler_params=pltpu.CompilerParams(
            collective_id=2, has_side_effects=True, vmem_limit_bytes=VMEM_LIMIT
        ),
        name="conv_backward",
    )(padded, dil, weight, *saved)


def on_device(
    out_cot,
    mix_weight,
    corr_kernels,
    momentum,
    spin_up,
    layer_input,
    pre_one,
    pre_two,
    conv_weight,
    dilation,
):
    chan_block = out_cot.shape[1]
    site_count = out_cot.shape[2]
    side = corr_kernels.shape[3]
    n = lax.axis_size("chan")
    slab = layer_input.shape[2]
    gate = jnp.where(spin_up == 1, 1.5, 0.5).astype(jnp.float32)
    gate = jnp.broadcast_to(gate, (8, slab))
    input_cot, gates = mix(n, out_cot[0], gate, mix_weight.T)
    gates = gates[:, 0, :].reshape(1, side, side)
    picked = lax.dynamic_index_in_dim(corr_kernels, momentum[0], axis=1, keepdims=False)
    positions = jnp.arange(side, dtype=jnp.int32)
    circ_table = (
        (positions[None, :] - positions[:, None]) % side == positions[:, None, None]
    ).astype(jnp.float32)
    circulant = jnp.einsum(
        "aci,ixy->acxy", picked, circ_table, precision=lax.Precision.HIGHEST
    )
    grid_values = input_cot.astype(jnp.float32).reshape(chan_block, side, side)
    high = lax.Precision.HIGH
    halfway = jnp.einsum("cxX,cxy->cXy", circulant[0], grid_values, precision=high)
    corr_grad = jnp.einsum("cXy,cyY->cXY", halfway, circulant[1], precision=high)
    corr_grad = corr_grad.astype(jnp.bfloat16).astype(jnp.float32)
    gated = (corr_grad * gates).astype(jnp.bfloat16).reshape(chan_block, site_count)
    padded = regroup(n, gated)
    norm = 1.0 / math.sqrt(out_cot.shape[0] * lax.axis_size("samp") * site_count)
    saved = (layer_input[0], pre_one[0], pre_two[0])
    result, weight_grad = backward(
        n, lax.axis_size("samp"), norm, padded, dilation, conv_weight, saved
    )
    return (result[None], weight_grad)


def solution(mesh):
    in_specs = (
        P("samp", "chan", None),
        P(),
        P(None, None, "chan", None),
        P("samp"),
        P("samp", "chan"),
        P("samp", None, "chan"),
        P("samp", None, "chan"),
        P("samp", None, "chan"),
        P(),
        P(),
    )
    out_specs = (P("samp", None, "chan"), P(None, None, "chan", None))
    return jax.shard_map(
        on_device, mesh=mesh, in_specs=in_specs, out_specs=out_specs, check_vma=False
    )
```
